32 devices in a mesh: req: 8 (over z, y), mdl: 4 (over x, core).
Axes of the slice: x: 2, y: 2, z: 4, core: 2. Of those that a mesh axis runs over, the one named last changes fastest.
Arguments:
- tokens: bfloat16 [2048, 1024], P('req', 'mdl'), may hold values from -6 to 6
- perm: int32 [32], replicated, may hold values from 0 to 31, each once
- w_query: bfloat16 [1024, 1024], P(None, 'mdl'), may hold values from -0.1875 to 0.1875
- q_bias: bfloat16 [1024], P('mdl'), may hold values from -6 to 6
- w_key: bfloat16 [1024, 1024], P(None, 'mdl'), may hold values from -0.1875 to 0.1875
- w_value: bfloat16 [1024, 1024], P(None, 'mdl'), may hold values from -0.1875 to 0.1875
- w_out: bfloat16 [1024, 1024], P('mdl'), may hold values from -0.1875 to 0.1875
- norm_gain: float32 [1024], P('mdl'), may hold values from 0.5 to 1.5
- norm_bias: float32 [1024], P('mdl'), may hold values from -3 to 3
- w_fc1: bfloat16 [1024, 2048], P(None, 'mdl'), may hold values from -0.1875 to 0.1875
- fc1_bias: float32 [2048], P('mdl'), may hold values from -4 to 4
- w_fc2: bfloat16 [2048, 1024], P('mdl'), may hold values from -0.125 to 0.125
- fc2_bias: float32 [1024], P('mdl'), may hold values from -3 to 3
- final_gain: float32 [1024], P('mdl'), may hold values from 0.5 to 1.5
- final_bias: float32 [1024], P('mdl'), may hold values from -3 to 3
- key_pool: bfloat16 [56, 128, 1024], P('req', None, 'mdl'), may hold values from -1000 to 1000
- value_pool: bfloat16 [56, 128, 1024], P('req', None, 'mdl'), may hold values from -6 to 6
- page_table: int32 [32, 4], P('req'), may hold values from 0 to 55, as said below
- cache_len: int32 [32], P('req'), may hold values from 1 to 512, as said below
- parents: int32 [32, 64], P('req'), may hold values from -1 to 62, as said below
- accepted: int32 [32, 8], P('req'), may hold values from 0 to 63
Outputs:
- layer_out: bfloat16 [2048, 1024], P('req', 'mdl')
- kept_keys: bfloat16 [32, 8, 1024], P('req', None, 'mdl')
- kept_values: bfloat16 [32, 8, 1024], P('req', None, 'mdl')
The draws below stay inside these ranges and needn't reach their ends.
Inputs may be any that keep to these rules, and one draw needn't show every extreme that they name: `page_table`: every entry of row s names a page held by index s // 4 of req, that is one of pages (s // 4) * 7 to (s // 4) * 7 + 6; the pages that the slots of one index of req use are distinct. `cache_len`: the lengths of the slots of one index of req use at most 7 pages together. parents[s, 0] = -1 and 0 <= parents[s, i] < i for i > 0.
All inputs are finite; a program needn't handle non-finite values.
Results may differ from the reference program's by a relative error of at most 0.01.
Values may be sent and summed in bfloat16 or wider, within the bound.
A program may use at most 64 MiB of HBM per device.

```python
import jax
import jax.numpy as jnp
from jax import lax

D = 1024
HEADS = 16
HD = 64
FF = 2048
DRAFT = 64
ACCEPT = 8
PAGE = 128
MAXPAGES = 4
REQ_DEV = 4
PAGES_DEV = 7
REQUESTS = 32
TOKENS = 2048
PAGES_ALL = 56
N_MDL = 4


def bias_vector(key):
    return jnp.clip(jax.random.normal(jax.random.fold_in(key, 11), (D,), jnp.float32), -5.5, 5.5)


def draw_q_bias(key, part):
    return bias_vector(key).astype(jnp.bfloat16)


def draw_key_pool(key, part):
    pool_shape = (PAGES_ALL, PAGE, D)
    noise_key = jax.random.fold_in(key, 31)
    entries = jnp.clip(jax.random.normal(noise_key, pool_shape, jnp.float32), -6.0, 6.0)
    return entries.astype(jnp.bfloat16)


def cache_layout(key):
    base_key = jax.random.fold_in(key, 23)
    count_key, forced_key, tail_key, order_key = jax.random.split(base_key, 4)
    dev_count = REQUESTS // REQ_DEV
    raw_pages = jax.random.randint(count_key, (dev_count, REQ_DEV), 1, MAXPAGES + 1)
    forced_dev = jax.random.randint(forced_key, (), 0, dev_count)
    raw_pages = raw_pages.at[forced_dev, 0].set(MAXPAGES)
    spare_pages = PAGES_DEV - REQ_DEV
    extra_pages = raw_pages - 1
    earlier = jnp.cumsum(extra_pages, axis=1) - extra_pages
    page_counts = 1 + jnp.clip(jnp.minimum(extra_pages, spare_pages - earlier), 0, None)
    tail_len = jax.random.randint(tail_key, (dev_count, REQ_DEV), 1, PAGE + 1)
    lengths = (page_counts - 1) * PAGE + tail_len
    lengths = lengths.at[forced_dev, 0].set(MAXPAGES * PAGE)
    order_keys = jax.random.split(order_key, dev_count)
    page_order = jax.vmap(lambda one_key: jax.random.permutation(one_key, PAGES_DEV))(order_keys).astype(jnp.int32)
    starts = jnp.cumsum(page_counts, axis=1) - page_counts
    positions = (starts[:, :, None] + jnp.arange(MAXPAGES, dtype=jnp.int32)[None, None, :]) % PAGES_DEV
    local_pages = jnp.take_along_axis(jnp.broadcast_to(page_order[:, None, :], (dev_count, REQ_DEV, PAGES_DEV)), positions, axis=2)
    global_pages = local_pages + (jnp.arange(dev_count, dtype=jnp.int32) * PAGES_DEV)[:, None, None]
    return (lengths.reshape(REQUESTS).astype(jnp.int32), global_pages.reshape(REQUESTS, MAXPAGES).astype(jnp.int32))


def draw_cache_len(key, part):
    return cache_layout(key)[0]


def draw_page_table(key, part):
    return cache_layout(key)[1]


def draw_parents(key, part):
    limits = jnp.maximum(jnp.arange(DRAFT, dtype=jnp.int32), 1)
    picks = jax.random.randint(jax.random.fold_in(key, 41), (REQUESTS, DRAFT), 0, limits)
    picks = jnp.where(jnp.arange(DRAFT) == 0, -1, picks)
    picks = picks.at[0, DRAFT - 1].set(DRAFT - 2)
    return picks.astype(jnp.int32)


def place_ends(values, own_key, smallest, top_value):
    shape = values.shape
    spot = [jax.random.randint(jax.random.fold_in(own_key, axis), (), 0, shape[axis]) for axis in range(len(shape))]
    values = values.at[tuple(spot)].set(smallest)
    longest = shape.index(max(shape))
    spot[longest] = (spot[longest] + 1) % shape[longest]
    return values.at[tuple(spot)].set(top_value)


def levels(key, dims, cuts, low, high):
    def one(position, parts):
        draws = jax.random.uniform(jax.random.fold_in(jax.random.fold_in(key, 6), position), (parts,), jnp.float32, low / len(cuts), high / len(cuts))
        return jnp.repeat(jnp.exp(draws), dims[position] // parts).reshape((-1,) + (1,) * (len(dims) - position - 1))

    level = one(*cuts[0])
    for cut in cuts[1:]:
        level = level * one(*cut)
    return level


def normal_values(own_key, shape, width, most, cuts=(), kind=jnp.bfloat16):
    result = width * jax.random.normal(own_key, shape, jnp.float32)
    if cuts:
        result = result * levels(own_key, shape, cuts, -0.22, 0.18)
    return jnp.clip(result, -most, most).astype(kind)


def setup_inputs(seed: int = 0) -> dict:
    arg_keys = jax.random.split(jax.random.key(seed), 22)
    tokens = normal_values(arg_keys[0], (TOKENS, D), 1.0, 6.0, ((0, 8), (1, 4)))
    perm = jax.random.permutation(arg_keys[1], REQUESTS).astype(jnp.int32)
    w_query = normal_values(arg_keys[2], (D, D), D ** -0.5, 0.1875, ((1, 4),))
    q_bias = draw_q_bias(jax.random.fold_in(arg_keys[21], 71), 0)
    w_key = normal_values(arg_keys[4], (D, D), D ** -0.5, 0.1875, ((1, 4),))
    w_value = normal_values(arg_keys[5], (D, D), D ** -0.5, 0.1875, ((1, 4),))
    w_out = normal_values(arg_keys[6], (D, D), D ** -0.5, 0.1875, ((0, 4),))
    norm_gain = jnp.clip(1.0 + 0.1 * jax.random.normal(arg_keys[7], (D,), jnp.float32), 0.5, 1.5)
    norm_bias = normal_values(arg_keys[8], (D,), 0.5, 3.0, ((0, 4),), jnp.float32)
    w_fc1 = normal_values(arg_keys[9], (D, FF), D ** -0.5, 0.1875, ((1, 4),))
    fc1_bias = normal_values(arg_keys[10], (FF,), 1.0, 4.0, ((0, 4),), jnp.float32)
    w_fc2 = normal_values(arg_keys[11], (FF, D), FF ** -0.5, 0.125, ((0, 4),))
    fc2_bias = normal_values(arg_keys[12], (D,), 0.5, 3.0, ((0, 4),), jnp.float32)
    final_gain = jnp.clip(1.0 + 0.1 * jax.random.normal(arg_keys[13], (D,), jnp.float32), 0.5, 1.5)
    final_bias = normal_values(arg_keys[14], (D,), 0.5, 3.0, ((0, 4),), jnp.float32)
    key_pool = draw_key_pool(jax.random.fold_in(arg_keys[21], 71), 0)
    value_pool = normal_values(arg_keys[16], (PAGES_ALL, PAGE, D), 1.0, 6.0, ((0, 8), (2, 4)))
    page_table = draw_page_table(jax.random.fold_in(arg_keys[21], 71), 0)
    cache_len = draw_cache_len(jax.random.fold_in(arg_keys[21], 71), 0)
    parents = draw_parents(jax.random.fold_in(arg_keys[21], 71), 0)
    accepted = place_ends(jax.random.randint(arg_keys[20], (REQUESTS, ACCEPT), 0, DRAFT), jax.random.fold_in(arg_keys[20], 1), 0, DRAFT - 1).astype(jnp.int32)
    return dict(tokens=tokens, perm=perm, w_query=w_query, q_bias=q_bias, w_key=w_key, w_value=w_value, w_out=w_out, norm_gain=norm_gain, norm_bias=norm_bias, w_fc1=w_fc1, fc1_bias=fc1_bias, w_fc2=w_fc2, fc2_bias=fc2_bias, final_gain=final_gain, final_bias=final_bias, key_pool=key_pool, value_pool=value_pool, page_table=page_table, cache_len=cache_len, parents=parents, accepted=accepted)


def ancestry(parents):
    draft_len = parents.shape[-1]
    node_ids = jnp.arange(draft_len, dtype=jnp.int32)
    hop_matrix = (parents[..., :, None] == node_ids).astype(jnp.float32)
    reached = jnp.broadcast_to(jnp.eye(draft_len, dtype=jnp.float32), hop_matrix.shape)
    for doubling in range((draft_len - 1).bit_length()):
        reached = jnp.minimum(reached + jnp.einsum('rij,rjk->rik', reached, hop_matrix), 1.0)
        hop_matrix = jnp.minimum(jnp.einsum('rij,rjk->rik', hop_matrix, hop_matrix), 1.0)
    return reached > 0.5

def layer_norm(hidden, gain, bias):
    row_mean = lax.optimization_barrier(jnp.mean(hidden, axis=1))
    row_var = lax.optimization_barrier(jnp.mean(hidden * hidden, axis=1)) - row_mean * row_mean
    return ((hidden - row_mean[:, None]) * lax.rsqrt(row_var + 1e-05)[:, None] * gain + bias).astype(jnp.bfloat16)

def grouped_sum(start, left, right):
    group_width = left.shape[1] // N_MDL
    total = start
    for group in range(N_MDL):
        partial_value = jnp.dot(left[:, group * group_width:(group + 1) * group_width], right[group * group_width:(group + 1) * group_width], preferred_element_type=jnp.float32).astype(jnp.bfloat16)
        partial_value = lax.optimization_barrier(partial_value)
        total = total + partial_value.astype(jnp.float32)
    return total

def reference(tokens, perm, w_query, q_bias, w_key, w_value, w_out, norm_gain, norm_bias, w_fc1, fc1_bias, w_fc2, fc2_bias, final_gain, final_bias, key_pool, value_pool, page_table, cache_len, parents, accepted):
    by_position = tokens.reshape(DRAFT, REQUESTS, D)
    served_x = jnp.transpose(by_position[:, perm], (1, 0, 2)).reshape(REQUESTS * DRAFT, D)
    query = (jnp.dot(served_x, w_query, preferred_element_type=jnp.float32) + q_bias.astype(jnp.float32)).astype(jnp.bfloat16)
    keys_new = jnp.dot(served_x, w_key, preferred_element_type=jnp.float32).astype(jnp.bfloat16)
    values_new = jnp.dot(served_x, w_value, preferred_element_type=jnp.float32).astype(jnp.bfloat16)
    ancestors = ancestry(parents)
    score_scale = HD ** (-0.5)
    span_len = MAXPAGES * PAGE

    def one_slot(inputs):
        slot_query, slot_keys, slot_values, pages_row, length, tree_mask = inputs
        cache_keys = key_pool[pages_row].reshape(span_len, HEADS, HD).astype(jnp.float32)
        cache_values = value_pool[pages_row].reshape(span_len, HEADS, HD).astype(jnp.float32)
        query_heads = slot_query.reshape(DRAFT, HEADS, HD).astype(jnp.float32)
        draft_keys = slot_keys.reshape(DRAFT, HEADS, HD).astype(jnp.float32)
        draft_values = slot_values.reshape(DRAFT, HEADS, HD).astype(jnp.float32)
        cache_scores = jnp.einsum('qhe,khe->hqk', query_heads, cache_keys) * score_scale
        draft_scores = jnp.einsum('qhe,khe->hqk', query_heads, draft_keys) * score_scale
        in_range = jnp.arange(span_len) < length
        cache_scores = jnp.where(in_range[None, None, :], cache_scores, -1e+30)
        draft_scores = jnp.where(tree_mask[None, :, :], draft_scores, -1e+30)
        highest = jnp.maximum(cache_scores.max(-1), draft_scores.max(-1))[..., None]
        cache_weight = jnp.exp(cache_scores - highest)
        draft_weight = jnp.exp(draft_scores - highest)
        weight_sum = cache_weight.sum(-1, keepdims=True) + draft_weight.sum(-1, keepdims=True)
        cache_probs = (cache_weight / weight_sum).astype(jnp.bfloat16).astype(jnp.float32)
        draft_probs = (draft_weight / weight_sum).astype(jnp.bfloat16).astype(jnp.float32)
        all_probs = jnp.concatenate([cache_probs, draft_probs], axis=-1)
        all_values = jnp.concatenate([cache_values, draft_values], axis=0)
        mixed = jnp.einsum('hqk,khe->qhe', all_probs, all_values)
        return mixed.reshape(DRAFT, D).astype(jnp.bfloat16)
    attended = lax.map(one_slot, (query.reshape(REQUESTS, DRAFT, D), keys_new.reshape(REQUESTS, DRAFT, D), values_new.reshape(REQUESTS, DRAFT, D), page_table, cache_len, ancestors))
    attended = attended.reshape(REQUESTS * DRAFT, D)
    hidden = grouped_sum(served_x.astype(jnp.float32), attended, w_out)
    normed_first = layer_norm(hidden, norm_gain, norm_bias)
    inner = jnp.dot(normed_first, w_fc1, preferred_element_type=jnp.float32) + fc1_bias
    activated = jax.nn.gelu(inner, approximate=False).astype(jnp.bfloat16)
    second_hidden = grouped_sum(normed_first.astype(jnp.float32), activated, w_fc2) + fc2_bias
    normed = layer_norm(second_hidden, final_gain, final_bias)
    normed = jnp.transpose(normed.reshape(REQUESTS, DRAFT, D), (1, 0, 2))
    layer_out = jnp.zeros((DRAFT, REQUESTS, D), jnp.bfloat16).at[:, perm].set(normed).reshape(TOKENS, D)
    kept_keys = jnp.take_along_axis(keys_new.reshape(REQUESTS, DRAFT, D), accepted[:, :, None], axis=1)
    kept_values = jnp.take_along_axis(values_new.reshape(REQUESTS, DRAFT, D), accepted[:, :, None], axis=1)
    return (layer_out, kept_keys, kept_values)
```

```python
import functools

import jax
import jax.numpy as jnp
from jax import lax
from jax.experimental import pallas as pl
from jax.experimental.pallas import tpu as pltpu
from jax.sharding import PartitionSpec as P

HD = 64


def ancestry(parents):
    draft_len = parents.shape[-1]
    node_ids = jnp.arange(draft_len, dtype=jnp.int32)
    hop_matrix = (parents[..., :, None] == node_ids).astype(jnp.bfloat16)
    reached = jnp.broadcast_to(jnp.eye(draft_len, dtype=jnp.bfloat16), hop_matrix.shape)
    for doubling in range((draft_len - 1).bit_length()):
        grown = jnp.einsum("rij,rjk->rik", reached, hop_matrix, preferred_element_type=jnp.float32)
        squared = jnp.einsum(
            "rij,rjk->rik", hop_matrix, hop_matrix, preferred_element_type=jnp.float32
        )
        reached = jnp.minimum(reached.astype(jnp.float32) + grown, 1.0).astype(jnp.bfloat16)
        hop_matrix = jnp.minimum(squared, 1.0).astype(jnp.bfloat16)
    return reached > 0.5


def outgoing_rows(perm, rows_dev, req_count, my_index):
    requests = perm.shape[0]
    per_dev = requests // req_count
    block_count = max(1, rows_dev // requests)
    target = jnp.arange(req_count, dtype=jnp.int32)[:, None, None]
    lane_index = jnp.arange(per_dev, dtype=jnp.int32)[None, :, None]
    offset = jnp.arange(block_count, dtype=jnp.int32)[None, None, :]
    request = perm[target * per_dev + lane_index]
    first_pos = my_index * rows_dev // requests
    local_row = (first_pos + offset) * requests + request - my_index * rows_dev
    usable = (local_row >= 0) & (local_row < rows_dev)
    return (jnp.clip(local_row, 0, rows_dev - 1).reshape(-1), usable.reshape(-1))


def incoming_rows(perm, rows_dev, req_count, my_index, draft_len):
    requests = perm.shape[0]
    per_dev = requests // req_count
    block_count = max(1, rows_dev // requests)
    slot_count = per_dev * block_count
    lane_index = jnp.arange(per_dev, dtype=jnp.int32)[:, None]
    position = jnp.arange(draft_len, dtype=jnp.int32)[None, :]
    request = perm[my_index * per_dev + lane_index]
    flat_pos = position * requests + request
    source = flat_pos // rows_dev
    offset = flat_pos % rows_dev // requests
    return (source * slot_count + lane_index * block_count + offset).reshape(-1)


def returning_rows(perm, rows_dev, req_count, my_index, draft_len):
    requests = perm.shape[0]
    per_dev = requests // req_count
    block_count = max(1, rows_dev // requests)
    source = jnp.arange(req_count, dtype=jnp.int32)[:, None, None]
    lane_index = jnp.arange(per_dev, dtype=jnp.int32)[None, :, None]
    offset = jnp.arange(block_count, dtype=jnp.int32)[None, None, :]
    request = perm[my_index * per_dev + lane_index]
    position = source * rows_dev // requests + offset
    usable = ((position * requests + request) // rows_dev == source) & (position < draft_len)
    row_index = lane_index * draft_len + jnp.clip(position, 0, draft_len - 1)
    return (row_index.reshape(-1), usable.reshape(-1))


def arriving_rows(perm, rows_dev, req_count, my_index):
    requests = perm.shape[0]
    per_dev = requests // req_count
    block_count = max(1, rows_dev // requests)
    slot_count = per_dev * block_count
    inverse = jnp.zeros((requests,), jnp.int32).at[perm].set(jnp.arange(requests, dtype=jnp.int32))
    local_row = jnp.arange(rows_dev, dtype=jnp.int32)
    request = (my_index * rows_dev + local_row) % requests
    slot_of = inverse[request]
    offset = local_row // requests
    return slot_of // per_dev * slot_count + slot_of % per_dev * block_count + offset


def attend(query, keys_new, values_new, key_pool, value_pool, local_pages, cache_len, parents):
    per_dev, draft_len, part_width = query.shape
    head_count = part_width // HD
    cache_keys = jnp.transpose(
        key_pool[local_pages].reshape(per_dev, -1, head_count, HD), (0, 2, 1, 3)
    )
    cache_values = jnp.transpose(
        value_pool[local_pages].reshape(per_dev, -1, head_count, HD), (0, 2, 1, 3)
    )
    key_span = cache_keys.shape[2]
    query_heads = jnp.transpose(query.reshape(per_dev, draft_len, head_count, HD), (0, 2, 1, 3))
    draft_keys = jnp.transpose(keys_new.reshape(per_dev, draft_len, head_count, HD), (0, 2, 1, 3))
    draft_values = jnp.transpose(
        values_new.reshape(per_dev, draft_len, head_count, HD), (0, 2, 1, 3)
    )
    score_scale = HD ** (-0.5)
    cache_scores = (
        jnp.einsum("rhqe,rhke->rhqk", query_heads, cache_keys, preferred_element_type=jnp.float32)
        * score_scale
    )
    draft_scores = (
        jnp.einsum("rhqe,rhke->rhqk", query_heads, draft_keys, preferred_element_type=jnp.float32)
        * score_scale
    )
    in_range = jnp.arange(key_span, dtype=jnp.int32)[None, :] < cache_len[:, None]
    tree_mask = ancestry(parents)
    cache_scores = jnp.where(in_range[:, None, None, :], cache_scores, -1e30)
    draft_scores = jnp.where(tree_mask[:, None, :, :], draft_scores, -1e30)
    highest = jnp.maximum(cache_scores.max(-1), draft_scores.max(-1))[..., None]
    cache_weight = jnp.exp(cache_scores - highest)
    draft_weight = jnp.exp(draft_scores - highest)
    weight_sum = cache_weight.sum(-1, keepdims=True) + draft_weight.sum(-1, keepdims=True)
    cache_probs = (cache_weight / weight_sum).astype(jnp.bfloat16)
    draft_probs = (draft_weight / weight_sum).astype(jnp.bfloat16)
    mixed = jnp.einsum(
        "rhqk,rhke->rhqe", cache_probs, cache_values, preferred_element_type=jnp.float32
    )
    mixed = mixed + jnp.einsum(
        "rhqk,rhke->rhqe", draft_probs, draft_values, preferred_element_type=jnp.float32
    )
    mixed = jnp.transpose(mixed, (0, 2, 1, 3))
    return mixed.reshape(per_dev, draft_len, part_width).astype(jnp.bfloat16)


def fold_features(row_part, weights):
    piece = lax.all_gather(row_part, "mdl", axis=1, tiled=True)
    return tuple((jnp.dot(piece, weight, preferred_element_type=jnp.float32) for weight in weights))


def reduce_groups(partial_value):
    return lax.psum_scatter(
        partial_value.astype(jnp.bfloat16), "mdl", scatter_dimension=1, tiled=True
    ).astype(jnp.float32)


def normalize(hidden, gain, bias):
    full_width = hidden.shape[1] * lax.axis_size("mdl")
    sum_first, sum_second = lax.psum(
        (jnp.sum(hidden, axis=1), jnp.sum(hidden * hidden, axis=1)), "mdl"
    )
    row_mean = sum_first / full_width
    row_var = sum_second / full_width - row_mean * row_mean
    return (
        (hidden - row_mean[:, None]) * lax.rsqrt(row_var + 1e-05)[:, None] * gain + bias
    ).astype(jnp.bfloat16)


def per_device_general(
    tokens,
    perm,
    w_query,
    q_bias,
    w_key,
    w_value,
    w_out,
    norm_gain,
    norm_bias,
    w_fc1,
    fc1_bias,
    w_fc2,
    fc2_bias,
    final_gain,
    final_bias,
    key_pool,
    value_pool,
    page_table,
    cache_len,
    parents,
    accepted,
):
    req_count = lax.axis_size("req")
    my_index = lax.axis_index("req")
    rows_dev, part_width = tokens.shape
    per_dev, draft_len = parents.shape
    pages_dev = key_pool.shape[0]
    send_rows, send_usable = outgoing_rows(perm, rows_dev, req_count, my_index)
    take_rows = incoming_rows(perm, rows_dev, req_count, my_index, draft_len)
    back_rows, back_usable = returning_rows(perm, rows_dev, req_count, my_index, draft_len)
    home_rows = arriving_rows(perm, rows_dev, req_count, my_index)
    slot_count = send_rows.shape[0] // req_count
    local_pages = page_table - my_index * pages_dev
    query_sum, key_sum, value_sum = fold_features(tokens, (w_query, w_key, w_value))
    query = (query_sum + q_bias.astype(jnp.float32)).astype(jnp.bfloat16)
    query, keys_new, values_new = (
        query,
        key_sum.astype(jnp.bfloat16),
        value_sum.astype(jnp.bfloat16),
    )
    packed = jnp.concatenate([query, keys_new, values_new], axis=1)
    outgoing = jnp.where(send_usable[:, None], packed[send_rows], 0).reshape(
        req_count, slot_count, 3 * part_width
    )
    arrived = lax.all_to_all(outgoing, "req", split_axis=0, concat_axis=0, tiled=True)
    served = arrived.reshape(req_count * slot_count, 3 * part_width)[take_rows].reshape(
        per_dev, draft_len, 3 * part_width
    )
    served_query = served[:, :, :part_width]
    served_keys = served[:, :, part_width : 2 * part_width]
    served_values = served[:, :, 2 * part_width :]
    attended = attend(
        served_query,
        served_keys,
        served_values,
        key_pool,
        value_pool,
        local_pages,
        cache_len,
        parents,
    )
    flat_rows = attended.reshape(per_dev * draft_len, part_width)
    back = jnp.where(back_usable[:, None], flat_rows[back_rows], 0).reshape(
        req_count, slot_count, part_width
    )
    returned = lax.all_to_all(back, "req", split_axis=0, concat_axis=0, tiled=True)
    home = returned.reshape(req_count * slot_count, part_width)[home_rows]
    summed = reduce_groups(jnp.dot(home, w_out, preferred_element_type=jnp.float32))
    normed_first = normalize(tokens.astype(jnp.float32) + summed, norm_gain, norm_bias)
    inner = fold_features(normed_first, (w_fc1,))[0]
    activated = jax.nn.gelu(inner + fc1_bias, approximate=False).astype(jnp.bfloat16)
    ff_summed = reduce_groups(jnp.dot(activated, w_fc2, preferred_element_type=jnp.float32))
    second_hidden = normed_first.astype(jnp.float32) + ff_summed + fc2_bias
    layer_out = normalize(second_hidden, final_gain, final_bias)
    kept_keys = jnp.take_along_axis(served_keys, accepted[:, :, None], axis=1)
    kept_values = jnp.take_along_axis(served_values, accepted[:, :, None], axis=1)
    return (layer_out, kept_keys, kept_values)


MESH = pl.DeviceIdType.MESH
NT = (((1,), (1,)), ((), ()))


def mm(left, right):
    return jnp.dot(left, right, preferred_element_type=jnp.float32)


def iota(shape, axis):
    return lax.broadcasted_iota(jnp.int32, shape, axis)


def fused_kernel(
    pages_dev,
    perm_ref,
    page_ref,
    len_ref,
    accepted_ref,
    parents_ref,
    q_bias_ref,
    gain1_ref,
    bias1_ref,
    fc1_bias_ref,
    fc2_bias_ref,
    gain2_ref,
    bias2_ref,
    tokens_hbm,
    wq_hbm,
    wk_hbm,
    wv_hbm,
    wo_hbm,
    w1_hbm,
    w2_hbm,
    keys_hbm,
    values_hbm,
    out_ref,
    kept_k_ref,
    kept_v_ref,
    tokens_v,
    wq_v,
    wk_v,
    wv_v,
    wo_v,
    w1_v,
    w2_v,
    keys_v,
    values_v,
    onehot_f,
    send1,
    recv1,
    x_all,
    params,
    acc_ref,
    q_ref,
    k_ref,
    v_ref,
    anc_ref,
    part_ref,
    recv2,
    nf_all,
    ff_ref,
    recv3,
    send5,
    recv5,
    load_sem,
    ssem1,
    rsem1,
    ssem_x,
    rsem_x,
    ssem_p,
    rsem_p,
    ssem2,
    rsem2,
    ssem_n,
    rsem_n,
    ssem3,
    rsem3,
    ssem5,
    rsem5,
):
    n_req = lax.axis_size("req")
    n_mdl = lax.axis_size("mdl")
    r = lax.axis_index("req")
    m = lax.axis_index("mdl")
    requests = perm_ref.shape[0]
    rows, width = tokens_v.shape
    draft = parents_ref.shape[1]
    per_dev = parents_ref.shape[0]
    pos_dev = rows // requests
    full = width * n_mdl

    core = m + 1 - 2 * (m % 2)
    across = (m + 2) % n_mdl
    diag = (core + 2) % n_mdl
    peers = (diag, across, core)

    loads = []
    for i, (source, target) in enumerate(
        (
            (tokens_hbm, tokens_v),
            (wq_hbm, wq_v),
            (wk_hbm, wk_v),
            (wv_hbm, wv_v),
            (keys_hbm, keys_v),
            (values_hbm, values_v),
            (wo_hbm, wo_v),
            (w1_hbm, w1_v),
            (w2_hbm, w2_v),
        )
    ):
        copy = pltpu.make_async_copy(source, target, load_sem.at[i])
        copy.start()
        loads.append(copy)

    barrier = pltpu.get_barrier_semaphore()
    others = [(i, j) for i in range(n_req) for j in range(n_mdl) if (i, j) != (0, 0)]
    for i, j in others:
        pl.semaphore_signal(
            barrier,
            inc=1,
            device_id=((r + i) % n_req, (m + j) % n_mdl),
            device_id_type=MESH,
        )

    block = (pos_dev, rows)
    place = iota(block, 1) - iota(block, 0) * requests
    for s in range(requests):
        onehot_f[s * pos_dev : (s + 1) * pos_dev, :] = (place == perm_ref[s]).astype(jnp.float32)
    onehot = onehot_f[...]
    loads[0].wait()
    packed = mm(onehot.astype(jnp.bfloat16), tokens_v[...]).astype(jnp.bfloat16)
    send1[...] = packed.reshape(send1.shape)

    params[m, 0:1, :] = gain1_ref[...]
    params[m, 1:2, :] = bias1_ref[...]
    params[m, 2:3, :] = fc2_bias_ref[...]
    params[m, 3:4, :] = gain2_ref[...]
    params[m, 4:5, :] = bias2_ref[...]
    params[m, 5:8, :] = jnp.zeros((3, width), jnp.float32)

    pl.semaphore_wait(barrier, len(others))

    copies1 = []
    for i in range(1, n_req):
        to = (r + i) % n_req
        copy = pltpu.make_async_remote_copy(
            src_ref=send1.at[to],
            dst_ref=recv1.at[r],
            send_sem=ssem1.at[i],
            recv_sem=rsem1.at[i],
            device_id=(to, m),
            device_id_type=MESH,
        )
        copy.start()
        copies1.append(copy)
    recv1[r] = send1[r]

    def push(source, target, ssem, rsem, i):
        copy = pltpu.make_async_remote_copy(
            src_ref=source,
            dst_ref=target,
            send_sem=ssem.at[i],
            recv_sem=rsem.at[i],
            device_id=(r, peers[i]),
            device_id_type=MESH,
        )
        copy.start()
        return copy

    copies_p = [push(params.at[m], params.at[m], ssem_p, rsem_p, i) for i in range(3)]

    square = (draft, draft)
    row_id, col_id = iota(square, 0), iota(square, 1)
    hops, reach = [], []
    for b in range(per_dev):
        line = jnp.broadcast_to(parents_ref[b : b + 1, :], square)
        column = jnp.sum(jnp.where(row_id == col_id, line, 0), axis=1, keepdims=True)
        hops.append((column == col_id).astype(jnp.bfloat16))
        reach.append((row_id == col_id).astype(jnp.float32))
    steps = (draft - 1).bit_length()
    for step in range(steps):
        for b in range(per_dev):
            hop = hops[b]
            reach[b] = jnp.minimum(reach[b] + mm(reach[b].astype(jnp.bfloat16), hop), 1.0)
            if step < steps - 1:
                hops[b] = jnp.minimum(mm(hop, hop), 1.0).astype(jnp.bfloat16)
    for b in range(per_dev):
        anc_ref[b] = reach[b]

    big = (rows, rows)
    n_id, c_id = iota(big, 0), iota(big, 1)
    lane, pos = n_id // draft, n_id % draft
    arrival = (pos // pos_dev) * (per_dev * pos_dev) + lane * pos_dev + pos % pos_dev
    reorder = (c_id == arrival).astype(jnp.float32).astype(jnp.bfloat16)
    home = jnp.transpose(onehot).astype(jnp.bfloat16)

    for copy in copies1:
        copy.wait()
    x_own = mm(reorder, recv1[...].reshape(rows, width)).astype(jnp.bfloat16)
    x_all[m] = x_own
    copies_x = [push(x_all.at[m], x_all.at[m], ssem_x, rsem_x, i) for i in range(3)]

    for i in (1, 2, 3):
        loads[i].wait()

    def project(which, first):
        part = x_all[which]
        span = pl.ds(pl.multiple_of(which * width, width), width)
        for j, weight in enumerate((wq_v, wk_v, wv_v)):
            value = mm(part, weight[span, :])
            if first:
                acc_ref[j] = value
            else:
                acc_ref[j] += value

    project(m, True)
    for i in (2, 1, 0):
        copies_x[i].wait()
        project(peers[i], False)
    q_ref[...] = (acc_ref[0] + q_bias_ref[...].astype(jnp.float32)).astype(jnp.bfloat16)
    k_ref[...] = acc_ref[1].astype(jnp.bfloat16)
    v_ref[...] = acc_ref[2].astype(jnp.bfloat16)

    for i in (4, 5, 6):
        loads[i].wait()

    heads = width // HD
    page_len = keys_v.shape[1]
    max_pages = page_ref.shape[1]
    head_lane = iota((draft, width), 1) // HD
    head_masks = [
        (head_lane == h).astype(jnp.float32).astype(jnp.bfloat16) for h in range(heads)
    ]
    key_id = iota((heads * draft, page_len), 1)
    scale = HD ** (-0.5)

    def attend_slot(b):
        span = pl.ds(pl.multiple_of(b * draft, draft), draft)
        slot_query = q_ref[span, :]
        stacked = jnp.concatenate([slot_query * mask for mask in head_masks], axis=0)
        length = len_ref[b]
        scores, values = [], []
        for t in range(max_pages):
            page = lax.rem(page_ref[b, t], pages_dev)
            part = lax.dot_general(stacked, keys_v[page], NT, preferred_element_type=jnp.float32)
            scores.append(jnp.where(key_id < length - t * page_len, part * scale, -1e30))
            values.append(values_v[page])
        part = lax.dot_general(stacked, k_ref[span, :], NT, preferred_element_type=jnp.float32)
        tree = jnp.concatenate([anc_ref[b]] * heads, axis=0)
        scores.append(jnp.where(tree > 0.5, part * scale, -1e30))
        values.append(v_ref[span, :])
        peak = functools.reduce(jnp.maximum, scores[:-1])
        peak = jnp.maximum(
            jnp.max(peak, axis=1, keepdims=True), jnp.max(scores[-1], axis=1, keepdims=True)
        )
        weights = [jnp.exp(part - peak) for part in scores]
        total = jnp.sum(sum(weights[1:-1], weights[0]), axis=1, keepdims=True)
        total = total + jnp.sum(weights[-1], axis=1, keepdims=True)
        inverse = 1.0 / total
        mixed = sum(
            mm((weight * inverse).astype(jnp.bfloat16), value)
            for weight, value in zip(weights, values)
        )
        result = jnp.zeros((draft, width), jnp.float32)
        for h in range(heads):
            result = jnp.where(head_lane == h, mixed[h * draft : (h + 1) * draft], result)
        return result.astype(jnp.bfloat16)

    copies2 = []
    for i, b in enumerate(peers):
        part_ref[b] = mm(attend_slot(b), wo_v[...]).astype(jnp.bfloat16)
        copies2.append(push(part_ref.at[b], recv2.at[m], ssem2, rsem2, i))
    recv2[m] = mm(attend_slot(m), wo_v[...]).astype(jnp.bfloat16)

    count = accepted_ref.shape[1]
    for b in range(per_dev):
        pick_row, pick_col = iota((count, rows), 0), iota((count, rows), 1)
        wanted = jnp.zeros((count, rows), jnp.int32)
        for a in range(count):
            wanted = jnp.where(pick_row == a, accepted_ref[b, a] + b * draft, wanted)
        pick = (pick_col == wanted).astype(jnp.float32).astype(jnp.bfloat16)
        kept_k_ref[b] = mm(pick, k_ref[...]).astype(jnp.bfloat16)
        kept_v_ref[b] = mm(pick, v_ref[...]).astype(jnp.bfloat16)

    for copy in copies_p:
        copy.wait()

    def vector(row):
        return jnp.concatenate([params[g, row : row + 1, :] for g in range(n_mdl)], axis=1)

    def layer_norm(hidden, gain, bias):
        mean = jnp.sum(hidden, axis=1, keepdims=True) / full
        var = jnp.sum(hidden * hidden, axis=1, keepdims=True) / full - mean * mean
        return (hidden - mean) * lax.rsqrt(var + 1e-05) * gain + bias

    own = pl.ds(pl.multiple_of(m * draft, draft), draft)
    hidden = jnp.concatenate([x_all[g, own, :] for g in range(n_mdl)], axis=1).astype(jnp.float32)
    for copy in copies2:
        copy.wait()
    for g in range(n_mdl):
        hidden = hidden + recv2[g].astype(jnp.float32)
    normed = layer_norm(hidden, vector(0), vector(1)).astype(jnp.bfloat16)
    nf_all[m] = normed
    copies_n = [push(nf_all.at[m], nf_all.at[m], ssem_n, rsem_n, i) for i in range(3)]
    loads[7].wait()
    loads[8].wait()

    def feed(pair):
        start = pl.multiple_of(pair * 2, 2)
        part = nf_all[pl.ds(start, 2)].reshape(2 * draft, full)
        inner = mm(part, w1_v[...]) + fc1_bias_ref[...]
        active = (0.5 * inner * (1.0 + lax.erf(inner * (0.5**0.5)))).astype(jnp.bfloat16)
        result = mm(active, w2_v[...]).astype(jnp.bfloat16)
        ff_ref[pl.ds(start, 2)] = result.reshape(2, draft, full)

    copies_n[2].wait()
    feed(m // 2)
    copies3 = [None] * 3
    copies3[2] = push(ff_ref.at[core], recv3.at[m], ssem3, rsem3, 2)
    copies_n[1].wait()
    copies_n[0].wait()
    feed(1 - m // 2)
    for i in (0, 1):
        copies3[i] = push(ff_ref.at[peers[i]], recv3.at[m], ssem3, rsem3, i)
    recv3[m] = ff_ref[m]
    second = normed.astype(jnp.float32) + vector(2)
    for copy in (copies3[2], copies3[1], copies3[0]):
        copy.wait()
    for g in range(n_mdl):
        second = second + recv3[g].astype(jnp.float32)
    final = layer_norm(second, vector(3), vector(4))
    for t in range(n_req):
        for g in range(n_mdl):
            send5[t, g] = final[
                t * pos_dev : (t + 1) * pos_dev, g * width : (g + 1) * width
            ].astype(jnp.bfloat16)
    me = r * n_mdl + m
    copies5 = []
    for n, (i, j) in enumerate(others):
        to_r, to_m = (r + i) % n_req, (m + j) % n_mdl
        copy = pltpu.make_async_remote_copy(
            src_ref=send5.at[to_r, to_m],
            dst_ref=recv5.at[me],
            send_sem=ssem5.at[n],
            recv_sem=rsem5.at[n],
            device_id=(to_r, to_m),
            device_id_type=MESH,
        )
        copy.start()
        copies5.append(copy)
    recv5[me] = send5[r, m]
    for copy in copies5:
        copy.wait()
    arrived = recv5[...].astype(jnp.float32).reshape(rows, width).astype(jnp.bfloat16)
    out_ref[...] = mm(home, arrived).astype(jnp.bfloat16)


def per_device_fused(
    tokens,
    perm,
    w_query,
    q_bias,
    w_key,
    w_value,
    w_out,
    norm_gain,
    norm_bias,
    w_fc1,
    fc1_bias,
    w_fc2,
    fc2_bias,
    final_gain,
    final_bias,
    key_pool,
    value_pool,
    page_table,
    cache_len,
    parents,
    accepted,
):
    n_req = lax.axis_size("req")
    n_mdl = lax.axis_size("mdl")
    rows, width = tokens.shape
    per_dev, draft = parents.shape
    full = width * n_mdl
    pos_dev = rows // perm.shape[0]
    smem = pl.BlockSpec(memory_space=pltpu.SMEM)
    vmem = pl.BlockSpec(memory_space=pltpu.VMEM)
    hbm = pl.BlockSpec(memory_space=pltpu.HBM)
    bf16, f32 = jnp.bfloat16, jnp.float32
    large = (tokens, w_query, w_key, w_value, w_out, w_fc1, w_fc2, key_pool, value_pool)
    n_all = n_req * n_mdl
    dma = pltpu.SemaphoreType.DMA
    kept = jax.ShapeDtypeStruct((per_dev, accepted.shape[1], width), bf16)
    return tuple(
        pl.pallas_call(
            functools.partial(fused_kernel, key_pool.shape[0]),
            out_shape=(jax.ShapeDtypeStruct((rows, width), bf16), kept, kept),
            in_specs=[smem] * 4 + [vmem] * 8 + [hbm] * 9,
            out_specs=(vmem, vmem, vmem),
            scratch_shapes=[pltpu.VMEM(a.shape, a.dtype) for a in large]
            + [
                pltpu.VMEM((rows, rows), f32),
                pltpu.VMEM((n_req, rows // n_req, width), bf16),
                pltpu.VMEM((n_req, rows // n_req, width), bf16),
                pltpu.VMEM((n_mdl, rows, width), bf16),
                pltpu.VMEM((n_mdl, 8, width), f32),
                pltpu.VMEM((3, rows, width), f32),
                pltpu.VMEM((rows, width), bf16),
                pltpu.VMEM((rows, width), bf16),
                pltpu.VMEM((rows, width), bf16),
                pltpu.VMEM((per_dev, draft, draft), f32),
                pltpu.VMEM((n_mdl, draft, full), bf16),
                pltpu.VMEM((n_mdl, draft, full), bf16),
                pltpu.VMEM((n_mdl, draft, full), bf16),
                pltpu.VMEM((n_mdl, draft, full), bf16),
                pltpu.VMEM((n_mdl, draft, full), bf16),
                pltpu.VMEM((n_req, n_mdl, pos_dev, width), bf16),
                pltpu.VMEM((n_all, pos_dev, width), bf16),
                dma((9,)),
                dma((n_req,)),
                dma((n_req,)),
                dma((3,)),
                dma((3,)),
                dma((3,)),
                dma((3,)),
                dma((3,)),
                dma((3,)),
                dma((3,)),
                dma((3,)),
                dma((3,)),
                dma((3,)),
                dma((n_all,)),
                dma((n_all,)),
            ],
            compiler_params=pltpu.CompilerParams(
                collective_id=0, has_side_effects=True, vmem_limit_bytes=56 * 2**20
            ),
        )(
            perm,
            page_table,
            cache_len,
            accepted,
            parents,
            q_bias[None, :],
            norm_gain[None, :],
            norm_bias[None, :],
            fc1_bias[None, :],
            fc2_bias[None, :],
            final_gain[None, :],
            final_bias[None, :],
            tokens,
            w_query,
            w_key,
            w_value,
            w_out,
            w_fc1,
            w_fc2,
            key_pool,
            value_pool,
        )
    )


def per_device(*args):
    rows, requests = args[0].shape[0], args[1].shape[0]
    per_dev, draft = args[19].shape
    n_mdl = lax.axis_size("mdl")
    whole_positions = rows % requests == 0 and rows // requests == 8
    if whole_positions and per_dev == n_mdl == 4 and per_dev * draft == rows:
        return per_device_fused(*args)
    return per_device_general(*args)


def solution(mesh):
    in_specs = (
        P("req", "mdl"),
        P(),
        P(None, "mdl"),
        P("mdl"),
        P(None, "mdl"),
        P(None, "mdl"),
        P("mdl", None),
        P("mdl"),
        P("mdl"),
        P(None, "mdl"),
        P("mdl"),
        P("mdl", None),
        P("mdl"),
        P("mdl"),
        P("mdl"),
        P("req", None, "mdl"),
        P("req", None, "mdl"),
        P("req", None),
        P("req"),
        P("req", None),
        P("req", None),
    )
    out_specs = (P("req", "mdl"), P("req", None, "mdl"), P("req", None, "mdl"))
    return jax.shard_map(
        per_device, mesh=mesh, in_specs=in_specs, out_specs=out_specs, check_vma=False
    )
```

```python
import functools

import jax
import jax.numpy as jnp
from jax import lax
from jax.experimental import pallas as pl
from jax.experimental.pallas import tpu as pltpu
from jax.sharding import PartitionSpec as P

HD = 64


def ancestry(parents):
    draft_len = parents.shape[-1]
    node_ids = jnp.arange(draft_len, dtype=jnp.int32)
    hop_matrix = (parents[..., :, None] == node_ids).astype(jnp.bfloat16)
    reached = jnp.broadcast_to(jnp.eye(draft_len, dtype=jnp.bfloat16), hop_matrix.shape)
    for doubling in range((draft_len - 1).bit_length()):
        grown = jnp.einsum("rij,rjk->rik", reached, hop_matrix, preferred_element_type=jnp.float32)
        squared = jnp.einsum(
            "rij,rjk->rik", hop_matrix, hop_matrix, preferred_element_type=jnp.float32
        )
        reached = jnp.minimum(reached.astype(jnp.float32) + grown, 1.0).astype(jnp.bfloat16)
        hop_matrix = jnp.minimum(squared, 1.0).astype(jnp.bfloat16)
    return reached > 0.5


def outgoing_rows(perm, rows_dev, req_count, my_index):
    requests = perm.shape[0]
    per_dev = requests // req_count
    block_count = max(1, rows_dev // requests)
    target = jnp.arange(req_count, dtype=jnp.int32)[:, None, None]
    lane_index = jnp.arange(per_dev, dtype=jnp.int32)[None, :, None]
    offset = jnp.arange(block_count, dtype=jnp.int32)[None, None, :]
    request = perm[target * per_dev + lane_index]
    first_pos = my_index * rows_dev // requests
    local_row = (first_pos + offset) * requests + request - my_index * rows_dev
    usable = (local_row >= 0) & (local_row < rows_dev)
    return (jnp.clip(local_row, 0, rows_dev - 1).reshape(-1), usable.reshape(-1))


def incoming_rows(perm, rows_dev, req_count, my_index, draft_len):
    requests = perm.shape[0]
    per_dev = requests // req_count
    block_count = max(1, rows_dev // requests)
    slot_count = per_dev * block_count
    lane_index = jnp.arange(per_dev, dtype=jnp.int32)[:, None]
    position = jnp.arange(draft_len, dtype=jnp.int32)[None, :]
    request = perm[my_index * per_dev + lane_index]
    flat_pos = position * requests + request
    source = flat_pos // rows_dev
    offset = flat_pos % rows_dev // requests
    return (source * slot_count + lane_index * block_count + offset).reshape(-1)


def returning_rows(perm, rows_dev, req_count, my_index, draft_len):
    requests = perm.shape[0]
    per_dev = requests // req_count
    block_count = max(1, rows_dev // requests)
    source = jnp.arange(req_count, dtype=jnp.int32)[:, None, None]
    lane_index = jnp.arange(per_dev, dtype=jnp.int32)[None, :, None]
    offset = jnp.arange(block_count, dtype=jnp.int32)[None, None, :]
    request = perm[my_index * per_dev + lane_index]
    position = source * rows_dev // requests + offset
    usable = ((position * requests + request) // rows_dev == source) & (position < draft_len)
    row_index = lane_index * draft_len + jnp.clip(position, 0, draft_len - 1)
    return (row_index.reshape(-1), usable.reshape(-1))


def arriving_rows(perm, rows_dev, req_count, my_index):
    requests = perm.shape[0]
    per_dev = requests // req_count
    block_count = max(1, rows_dev // requests)
    slot_count = per_dev * block_count
    inverse = jnp.zeros((requests,), jnp.int32).at[perm].set(jnp.arange(requests, dtype=jnp.int32))
    local_row = jnp.arange(rows_dev, dtype=jnp.int32)
    request = (my_index * rows_dev + local_row) % requests
    slot_of = inverse[request]
    offset = local_row // requests
    return slot_of // per_dev * slot_count + slot_of % per_dev * block_count + offset


def attend(query, keys_new, values_new, key_pool, value_pool, local_pages, cache_len, parents):
    per_dev, draft_len, part_width = query.shape
    head_count = part_width // HD
    cache_keys = jnp.transpose(
        key_pool[local_pages].reshape(per_dev, -1, head_count, HD), (0, 2, 1, 3)
    )
    cache_values = jnp.transpose(
        value_pool[local_pages].reshape(per_dev, -1, head_count, HD), (0, 2, 1, 3)
    )
    key_span = cache_keys.shape[2]
    query_heads = jnp.transpose(query.reshape(per_dev, draft_len, head_count, HD), (0, 2, 1, 3))
    draft_keys = jnp.transpose(keys_new.reshape(per_dev, draft_len, head_count, HD), (0, 2, 1, 3))
    draft_values = jnp.transpose(
        values_new.reshape(per_dev, draft_len, head_count, HD), (0, 2, 1, 3)
    )
    score_scale = HD ** (-0.5)
    cache_scores = (
        jnp.einsum("rhqe,rhke->rhqk", query_heads, cache_keys, preferred_element_type=jnp.float32)
        * score_scale
    )
    draft_scores = (
        jnp.einsum("rhqe,rhke->rhqk", query_heads, draft_keys, preferred_element_type=jnp.float32)
        * score_scale
    )
    in_range = jnp.arange(key_span, dtype=jnp.int32)[None, :] < cache_len[:, None]
    tree_mask = ancestry(parents)
    cache_scores = jnp.where(in_range[:, None, None, :], cache_scores, -1e30)
    draft_scores = jnp.where(tree_mask[:, None, :, :], draft_scores, -1e30)
    highest = jnp.maximum(cache_scores.max(-1), draft_scores.max(-1))[..., None]
    cache_weight = jnp.exp(cache_scores - highest)
    draft_weight = jnp.exp(draft_scores - highest)
    weight_sum = cache_weight.sum(-1, keepdims=True) + draft_weight.sum(-1, keepdims=True)
    cache_probs = (cache_weight / weight_sum).astype(jnp.bfloat16)
    draft_probs = (draft_weight / weight_sum).astype(jnp.bfloat16)
    mixed = jnp.einsum(
        "rhqk,rhke->rhqe", cache_probs, cache_values, preferred_element_type=jnp.float32
    )
    mixed = mixed + jnp.einsum(
        "rhqk,rhke->rhqe", draft_probs, draft_values, preferred_element_type=jnp.float32
    )
    mixed = jnp.transpose(mixed, (0, 2, 1, 3))
    return mixed.reshape(per_dev, draft_len, part_width).astype(jnp.bfloat16)


def fold_features(row_part, weights):
    piece = lax.all_gather(row_part, "mdl", axis=1, tiled=True)
    return tuple((jnp.dot(piece, weight, preferred_element_type=jnp.float32) for weight in weights))


def reduce_groups(partial_value):
    return lax.psum_scatter(
        partial_value.astype(jnp.bfloat16), "mdl", scatter_dimension=1, tiled=True
    ).astype(jnp.float32)


def normalize(hidden, gain, bias):
    full_width = hidden.shape[1] * lax.axis_size("mdl")
    sum_first, sum_second = lax.psum(
        (jnp.sum(hidden, axis=1), jnp.sum(hidden * hidden, axis=1)), "mdl"
    )
    row_mean = sum_first / full_width
    row_var = sum_second / full_width - row_mean * row_mean
    return (
        (hidden - row_mean[:, None]) * lax.rsqrt(row_var + 1e-05)[:, None] * gain + bias
    ).astype(jnp.bfloat16)


def per_device_general(
    tokens,
    perm,
    w_query,
    q_bias,
    w_key,
    w_value,
    w_out,
    norm_gain,
    norm_bias,
    w_fc1,
    fc1_bias,
    w_fc2,
    fc2_bias,
    final_gain,
    final_bias,
    key_pool,
    value_pool,
    page_table,
    cache_len,
    parents,
    accepted,
):
    req_count = lax.axis_size("req")
    my_index = lax.axis_index("req")
    rows_dev, part_width = tokens.shape
    per_dev, draft_len = parents.shape
    pages_dev = key_pool.shape[0]
    send_rows, send_usable = outgoing_rows(perm, rows_dev, req_count, my_index)
    take_rows = incoming_rows(perm, rows_dev, req_count, my_index, draft_len)
    back_rows, back_usable = returning_rows(perm, rows_dev, req_count, my_index, draft_len)
    home_rows = arriving_rows(perm, rows_dev, req_count, my_index)
    slot_count = send_rows.shape[0] // req_count
    local_pages = page_table - my_index * pages_dev
    query_sum, key_sum, value_sum = fold_features(tokens, (w_query, w_key, w_value))
    query = (query_sum + q_bias.astype(jnp.float32)).astype(jnp.bfloat16)
    query, keys_new, values_new = (
        query,
        key_sum.astype(jnp.bfloat16),
        value_sum.astype(jnp.bfloat16),
    )
    packed = jnp.concatenate([query, keys_new, values_new], axis=1)
    outgoing = jnp.where(send_usable[:, None], packed[send_rows], 0).reshape(
        req_count, slot_count, 3 * part_width
    )
    arrived = lax.all_to_all(outgoing, "req", split_axis=0, concat_axis=0, tiled=True)
    served = arrived.reshape(req_count * slot_count, 3 * part_width)[take_rows].reshape(
        per_dev, draft_len, 3 * part_width
    )
    served_query = served[:, :, :part_width]
    served_keys = served[:, :, part_width : 2 * part_width]
    served_values = served[:, :, 2 * part_width :]
    attended = attend(
        served_query,
        served_keys,
        served_values,
        key_pool,
        value_pool,
        local_pages,
        cache_len,
        parents,
    )
    flat_rows = attended.reshape(per_dev * draft_len, part_width)
    back = jnp.where(back_usable[:, None], flat_rows[back_rows], 0).reshape(
        req_count, slot_count, part_width
    )
    returned = lax.all_to_all(back, "req", split_axis=0, concat_axis=0, tiled=True)
    home = returned.reshape(req_count * slot_count, part_width)[home_rows]
    summed = reduce_groups(jnp.dot(home, w_out, preferred_element_type=jnp.float32))
    normed_first = normalize(tokens.astype(jnp.float32) + summed, norm_gain, norm_bias)
    inner = fold_features(normed_first, (w_fc1,))[0]
    activated = jax.nn.gelu(inner + fc1_bias, approximate=False).astype(jnp.bfloat16)
    ff_summed = reduce_groups(jnp.dot(activated, w_fc2, preferred_element_type=jnp.float32))
    second_hidden = normed_first.astype(jnp.float32) + ff_summed + fc2_bias
    layer_out = normalize(second_hidden, final_gain, final_bias)
    kept_keys = jnp.take_along_axis(served_keys, accepted[:, :, None], axis=1)
    kept_values = jnp.take_along_axis(served_values, accepted[:, :, None], axis=1)
    return (layer_out, kept_keys, kept_values)


MESH = pl.DeviceIdType.MESH
NT = (((1,), (1,)), ((), ()))


def mm(left, right):
    return jnp.dot(left, right, preferred_element_type=jnp.float32)


def iota(shape, axis):
    return lax.broadcasted_iota(jnp.int32, shape, axis)


def fused_kernel(
    pages_dev,
    perm_ref,
    page_ref,
    len_ref,
    accepted_ref,
    parents_ref,
    q_bias_ref,
    gain1_ref,
    bias1_ref,
    fc1_bias_ref,
    fc2_bias_ref,
    gain2_ref,
    bias2_ref,
    tokens_hbm,
    wq_hbm,
    wk_hbm,
    wv_hbm,
    wo_hbm,
    w1_hbm,
    w2_hbm,
    keys_hbm,
    values_hbm,
    out_ref,
    kept_k_ref,
    kept_v_ref,
    tokens_v,
    wq_v,
    wk_v,
    wv_v,
    wo_v,
    w1_v,
    w2_v,
    keys_v,
    values_v,
    onehot_f,
    send1,
    x_all,
    params,
    acc_ref,
    q_ref,
    k_ref,
    v_ref,
    anc_ref,
    part_ref,
    recv2,
    nf_all,
    ff_ref,
    part3,
    recv3,
    send5,
    recv5,
    load_sem,
    ssem1,
    rsem1,
    ssem_x,
    rsem_x,
    ssem_p,
    rsem_p,
    ssem2,
    rsem2,
    ssem_n,
    rsem_n,
    ssem3,
    rsem3,
    ssem5,
    rsem5,
):
    n_req = lax.axis_size("req")
    n_mdl = lax.axis_size("mdl")
    r = lax.axis_index("req")
    m = lax.axis_index("mdl")
    requests = perm_ref.shape[0]
    rows, width = tokens_v.shape
    draft = parents_ref.shape[1]
    per_dev = parents_ref.shape[0]
    pos_dev = rows // requests
    full = width * n_mdl

    core = m + 1 - 2 * (m % 2)
    across = (m + 2) % n_mdl
    diag = (core + 2) % n_mdl
    peers = (diag, across, core)
    half = n_req // 2

    def place(source):
        return source % 2 * half + source // 2

    def position(row):
        group = row // pos_dev
        return (group % half * 2 + group // half) * pos_dev + row % pos_dev

    spot = place(r)

    loads = []
    for i, (source, target) in enumerate(
        (
            (tokens_hbm, tokens_v),
            (wq_hbm, wq_v),
            (wk_hbm, wk_v),
            (wv_hbm, wv_v),
            (keys_hbm, keys_v),
            (values_hbm, values_v),
            (wo_hbm, wo_v),
            (w1_hbm, w1_v),
            (w2_hbm, w2_v),
        )
    ):
        copy = pltpu.make_async_copy(source, target, load_sem.at[i])
        copy.start()
        loads.append(copy)

    barrier = pltpu.get_barrier_semaphore()
    others = [(i, 0) for i in range(1, n_req)] + [(0, j) for j in range(1, n_mdl)]
    for i, j in others:
        pl.semaphore_signal(
            barrier,
            inc=1,
            device_id=((r + i) % n_req, (m + j) % n_mdl),
            device_id_type=MESH,
        )

    block = (pos_dev, rows)
    local = iota(block, 1) - iota(block, 0) * requests
    for s in range(requests):
        onehot_f[s * pos_dev : (s + 1) * pos_dev, :] = (local == perm_ref[s]).astype(jnp.float32)
    onehot = onehot_f[...]
    loads[0].wait()
    packed = mm(onehot.astype(jnp.bfloat16), tokens_v[...])
    send1[...] = packed.reshape(send1.shape).astype(jnp.bfloat16)

    params[m, 0:1, :] = gain1_ref[...]
    params[m, 1:2, :] = bias1_ref[...]
    params[m, 2:3, :] = fc2_bias_ref[...]
    params[m, 3:4, :] = gain2_ref[...]
    params[m, 4:5, :] = bias2_ref[...]
    params[m, 5:8, :] = jnp.zeros((3, width), jnp.float32)

    pl.semaphore_wait(barrier, len(others))

    order = (1, n_req - 1, 2, n_req - 2, 3, n_req - 3, half)
    copies1 = []
    for i in order:
        to = (r + i) % n_req
        copy = pltpu.make_async_remote_copy(
            src_ref=send1.at[to],
            dst_ref=x_all.at[m, :, spot],
            send_sem=ssem1.at[i],
            recv_sem=rsem1.at[i],
            device_id=(to, m),
            device_id_type=MESH,
        )
        copy.start()
        copies1.append(copy)
    x_all[m, :, spot] = send1[r]

    def push(source, target, ssem, rsem, i, peer):
        copy = pltpu.make_async_remote_copy(
            src_ref=source,
            dst_ref=target,
            send_sem=ssem.at[i],
            recv_sem=rsem.at[i],
            device_id=(r, peer),
            device_id_type=MESH,
        )
        copy.start()
        return copy

    copies_p = [
        push(params.at[m], params.at[m], ssem_p, rsem_p, i, peer) for i, peer in enumerate(peers)
    ]

    square = (draft, draft)
    row_id, col_id = iota(square, 0), iota(square, 1)
    row_pos, col_pos = position(row_id), position(col_id)
    hops, reach = [], []
    for b in range(per_dev):
        line = jnp.broadcast_to(parents_ref[b : b + 1, :], square)
        column = jnp.sum(jnp.where(row_pos == col_id, line, 0), axis=1, keepdims=True)
        hops.append((column == col_pos).astype(jnp.bfloat16))
        reach.append((row_id == col_id).astype(jnp.float32))
    steps = (draft - 1).bit_length()
    for step in range(steps):
        for b in range(per_dev):
            hop = hops[b]
            reach[b] = jnp.minimum(reach[b] + mm(reach[b].astype(jnp.bfloat16), hop), 1.0)
            if step < steps - 1:
                hops[b] = jnp.minimum(mm(hop, hop), 1.0).astype(jnp.bfloat16)
    for b in range(per_dev):
        anc_ref[b] = reach[b]

    home = jnp.transpose(onehot).astype(jnp.bfloat16)

    far_x = []
    for i, copy in zip((0,) + order, [None] + copies1):
        if copy is not None:
            copy.wait_recv()
        piece = place((r + n_req - i) % n_req)
        far_x.append(
            push(x_all.at[m, :, piece], x_all.at[m, :, piece], ssem_x, rsem_x, i, across)
        )
    near_x = push(x_all.at[m], x_all.at[m], ssem_x, rsem_x, n_req, core)

    for i in (1, 2, 3):
        loads[i].wait()

    def project(which, first):
        part = x_all[which].astype(jnp.float32).reshape(rows, width).astype(jnp.bfloat16)
        span = pl.ds(pl.multiple_of(which * width, width), width)
        for j, weight in enumerate((wq_v, wk_v, wv_v)):
            value = mm(part, weight[span, :])
            if first:
                acc_ref[j] = value
            else:
                acc_ref[j] += value

    project(m, True)
    for copy in far_x:
        copy.wait()
    passed_x = push(x_all.at[across], x_all.at[across], ssem_x, rsem_x, n_req + 1, core)
    near_x.wait()
    project(core, False)
    project(across, False)
    passed_x.wait()
    project(diag, False)
    for copy in copies1:
        copy.wait_send()
    q_ref[...] = (acc_ref[0] + q_bias_ref[...].astype(jnp.float32)).astype(jnp.bfloat16)
    k_ref[...] = acc_ref[1].astype(jnp.bfloat16)
    v_ref[...] = acc_ref[2].astype(jnp.bfloat16)

    for i in (4, 5, 6):
        loads[i].wait()

    heads = width // HD
    page_len = keys_v.shape[1]
    max_pages = page_ref.shape[1]
    head_lane = iota((draft, width), 1) // HD
    head_masks = [
        (head_lane == h).astype(jnp.float32).astype(jnp.bfloat16) for h in range(heads)
    ]
    key_id = iota((heads * draft, page_len), 1)
    scale = HD ** (-0.5)

    def attend_slot(b):
        span = pl.ds(pl.multiple_of(b * draft, draft), draft)
        slot_query = q_ref[span, :]
        stacked = jnp.concatenate([slot_query * mask for mask in head_masks], axis=0)
        length = len_ref[b]
        scores, values = [], []
        for t in range(max_pages):
            page = lax.rem(page_ref[b, t], pages_dev)
            part = lax.dot_general(stacked, keys_v[page], NT, preferred_element_type=jnp.float32)
            scores.append(jnp.where(key_id < length - t * page_len, part * scale, -1e30))
            values.append(values_v[page])
        part = lax.dot_general(stacked, k_ref[span, :], NT, preferred_element_type=jnp.float32)
        tree = jnp.concatenate([anc_ref[b]] * heads, axis=0)
        scores.append(jnp.where(tree > 0.5, part * scale, -1e30))
        values.append(v_ref[span, :])
        peak = functools.reduce(jnp.maximum, scores[:-1])
        peak = jnp.maximum(
            jnp.max(peak, axis=1, keepdims=True), jnp.max(scores[-1], axis=1, keepdims=True)
        )
        weights = [jnp.exp(part - peak) for part in scores]
        total = jnp.sum(sum(weights[1:-1], weights[0]), axis=1, keepdims=True)
        total = total + jnp.sum(weights[-1], axis=1, keepdims=True)
        inverse = 1.0 / total
        mixed = sum(
            mm((weight * inverse).astype(jnp.bfloat16), value)
            for weight, value in zip(weights, values)
        )
        result = jnp.zeros((draft, width), jnp.float32)
        for h in range(heads):
            result = jnp.where(head_lane == h, mixed[h * draft : (h + 1) * draft], result)
        return result.astype(jnp.bfloat16)

    part_ref[0] = mm(attend_slot(diag), wo_v[...]).astype(jnp.bfloat16)
    mid2 = push(part_ref.at[0], recv2.at[0], ssem2, rsem2, 0, core)
    share = mm(attend_slot(across), wo_v[...])
    mid2.wait()
    part_ref[1] = (share + recv2[0].astype(jnp.float32)).astype(jnp.bfloat16)
    far2 = push(part_ref.at[1], recv2.at[1], ssem2, rsem2, 1, across)
    part_ref[2] = mm(attend_slot(core), wo_v[...]).astype(jnp.bfloat16)
    near2 = push(part_ref.at[2], recv2.at[2], ssem2, rsem2, 2, core)
    own_part = mm(attend_slot(m), wo_v[...]).astype(jnp.bfloat16).astype(jnp.float32)

    count = accepted_ref.shape[1]

    def slot_row(draft_pos):
        return place(draft_pos // pos_dev) * pos_dev + draft_pos % pos_dev

    for b in range(per_dev):
        pick_row, pick_col = iota((count, rows), 0), iota((count, rows), 1)
        wanted = jnp.zeros((count, rows), jnp.int32)
        for a in range(count):
            wanted = jnp.where(pick_row == a, slot_row(accepted_ref[b, a]) + b * draft, wanted)
        pick = (pick_col == wanted).astype(jnp.float32).astype(jnp.bfloat16)
        kept_k_ref[b] = mm(pick, k_ref[...]).astype(jnp.bfloat16)
        kept_v_ref[b] = mm(pick, v_ref[...]).astype(jnp.bfloat16)

    for copy in copies_p:
        copy.wait()

    def vector(row):
        return jnp.concatenate([params[g, row : row + 1, :] for g in range(n_mdl)], axis=1)

    def layer_norm(hidden, gain, bias):
        mean = jnp.sum(hidden, axis=1, keepdims=True) / full
        var = jnp.sum(hidden * hidden, axis=1, keepdims=True) / full - mean * mean
        return (hidden - mean) * lax.rsqrt(var + 1e-05) * gain + bias

    hidden = jnp.concatenate(
        [x_all[g, m].astype(jnp.float32).reshape(draft, width) for g in range(n_mdl)], axis=1
    )
    hidden = hidden + own_part
    near2.wait()
    hidden = hidden + recv2[2].astype(jnp.float32)
    far2.wait()
    hidden = hidden + recv2[1].astype(jnp.float32)
    normed = layer_norm(hidden, vector(0), vector(1)).astype(jnp.bfloat16)
    rows_k = draft // 2
    for k in range(2):
        nf_all[k, m] = normed[k * rows_k : (k + 1) * rows_k]
    far_n = [push(nf_all.at[k, m], nf_all.at[k, m], ssem_n, rsem_n, k, across) for k in range(2)]
    near_n = [push(nf_all.at[k, m], nf_all.at[k, m], ssem_n, rsem_n, 2 + k, core) for k in range(2)]
    passed_n = []
    loads[7].wait()
    loads[8].wait()
    second = normed.astype(jnp.float32) + vector(2)
    second = [second[:rows_k], second[rows_k:]]

    def pass_on(k):
        far_n[k].wait()
        block = nf_all.at[k, across]
        passed_n.append(push(block, block, ssem_n, rsem_n, 4 + k, core))

    def feed(k, pair):
        start = pl.multiple_of(pair * 2, 2)
        part = nf_all[k, pl.ds(start, 2)].reshape(2 * rows_k, full)
        inner = mm(part, w1_v[...]) + fc1_bias_ref[...]
        active = (0.5 * inner * (1.0 + lax.erf(inner * (0.5**0.5)))).astype(jnp.bfloat16)
        ff_ref[k] = mm(active, w2_v[...]).reshape(2, rows_k, full)

    def feed_near(k):
        near_n[k].wait()
        feed(k, m // 2)
        part3[k, 2] = ff_ref[k, core % 2].astype(jnp.bfloat16)
        second[k] = second[k] + ff_ref[k, m % 2].astype(jnp.bfloat16).astype(jnp.float32)
        return push(part3.at[k, 2], recv3.at[k, 2], ssem3, rsem3, 3 * k + 2, core)

    def feed_far(k):
        passed_n[k].wait()
        feed(k, 1 - m // 2)
        part3[k, 0] = ff_ref[k, diag % 2].astype(jnp.bfloat16)
        return push(part3.at[k, 0], recv3.at[k, 0], ssem3, rsem3, 3 * k, core)

    def cross(k, mid):
        mid.wait()
        total = ff_ref[k, across % 2] + recv3[k, 0].astype(jnp.float32)
        part3[k, 1] = total.astype(jnp.bfloat16)
        return push(part3.at[k, 1], recv3.at[k, 1], ssem3, rsem3, 3 * k + 1, across)

    me = r * n_mdl + m

    def finish(k, near, far):
        near.wait()
        hidden = second[k] + recv3[k, 2].astype(jnp.float32)
        far.wait()
        hidden = hidden + recv3[k, 1].astype(jnp.float32)
        final = layer_norm(hidden, vector(3), vector(4))
        for t in range(half):
            for g in range(n_mdl):
                send5[2 * t + k, g] = final[
                    t * pos_dev : (t + 1) * pos_dev, g * width : (g + 1) * width
                ].astype(jnp.bfloat16)
        for i in range(half):
            for j in range(n_mdl):
                to_r = (r // 2 + i) % half * 2 + k
                to_m = (m + j) % n_mdl
                copy = pltpu.make_async_remote_copy(
                    src_ref=send5.at[to_r, to_m],
                    dst_ref=recv5.at[me],
                    send_sem=ssem5,
                    recv_sem=rsem5,
                    device_id=(to_r, to_m),
                    device_id_type=MESH,
                )
                if i == 0 and j == 0:

                    @pl.when(r % 2 == k)
                    def _():
                        recv5[me] = send5[r, m]

                    @pl.when(r % 2 != k)
                    def _():
                        copy.start()

                else:
                    copy.start()

    pass_on(0)
    near_0 = feed_near(0)
    pass_on(1)
    mid_0 = feed_far(0)
    near_1 = feed_near(1)
    far_0 = cross(0, mid_0)
    mid_1 = feed_far(1)
    far_1 = cross(1, mid_1)
    finish(0, near_0, far_0)
    finish(1, near_1, far_1)
    n_others = n_req * n_mdl - 1
    pltpu.make_async_copy(recv5.at[:n_others], recv5.at[:n_others], ssem5).wait()
    pltpu.make_async_copy(recv5.at[:n_others], recv5.at[:n_others], rsem5).wait()
    arrived = recv5[...].astype(jnp.float32).reshape(rows, width).astype(jnp.bfloat16)
    out_ref[...] = mm(home, arrived).astype(jnp.bfloat16)


def per_device_fused(
    tokens,
    perm,
    w_query,
    q_bias,
    w_key,
    w_value,
    w_out,
    norm_gain,
    norm_bias,
    w_fc1,
    fc1_bias,
    w_fc2,
    fc2_bias,
    final_gain,
    final_bias,
    key_pool,
    value_pool,
    page_table,
    cache_len,
    parents,
    accepted,
):
    n_req = lax.axis_size("req")
    n_mdl = lax.axis_size("mdl")
    rows, width = tokens.shape
    per_dev, draft = parents.shape
    full = width * n_mdl
    pos_dev = rows // perm.shape[0]
    smem = pl.BlockSpec(memory_space=pltpu.SMEM)
    vmem = pl.BlockSpec(memory_space=pltpu.VMEM)
    hbm = pl.BlockSpec(memory_space=pltpu.HBM)
    bf16, f32 = jnp.bfloat16, jnp.float32
    large = (tokens, w_query, w_key, w_value, w_out, w_fc1, w_fc2, key_pool, value_pool)
    n_all = n_req * n_mdl
    dma = pltpu.SemaphoreType.DMA
    kept = jax.ShapeDtypeStruct((per_dev, accepted.shape[1], width), bf16)
    return tuple(
        pl.pallas_call(
            functools.partial(fused_kernel, key_pool.shape[0]),
            out_shape=(jax.ShapeDtypeStruct((rows, width), bf16), kept, kept),
            in_specs=[smem] * 4 + [vmem] * 8 + [hbm] * 9,
            out_specs=(vmem, vmem, vmem),
            scratch_shapes=[pltpu.VMEM(a.shape, a.dtype) for a in large]
            + [
                pltpu.VMEM((rows, rows), f32),
                pltpu.VMEM((n_req, per_dev, pos_dev, width), bf16),
                pltpu.VMEM((n_mdl, per_dev, n_req, pos_dev, width), bf16),
                pltpu.VMEM((n_mdl, 8, width), f32),
                pltpu.VMEM((3, rows, width), f32),
                pltpu.VMEM((rows, width), bf16),
                pltpu.VMEM((rows, width), bf16),
                pltpu.VMEM((rows, width), bf16),
                pltpu.VMEM((per_dev, draft, draft), f32),
                pltpu.VMEM((3, draft, full), bf16),
                pltpu.VMEM((3, draft, full), bf16),
                pltpu.VMEM((2, n_mdl, draft // 2, full), bf16),
                pltpu.VMEM((2, 2, draft // 2, full), f32),
                pltpu.VMEM((2, 3, draft // 2, full), bf16),
                pltpu.VMEM((2, 3, draft // 2, full), bf16),
                pltpu.VMEM((n_req, n_mdl, pos_dev, width), bf16),
                pltpu.VMEM((n_all, pos_dev, width), bf16),
                dma((9,)),
                dma((n_req,)),
                dma((n_req,)),
                dma((n_req + 2,)),
                dma((n_req + 2,)),
                dma((3,)),
                dma((3,)),
                dma((3,)),
                dma((3,)),
                dma((6,)),
                dma((6,)),
                dma((6,)),
                dma((6,)),
                dma,
                dma,
            ],
            compiler_params=pltpu.CompilerParams(
                collective_id=0, has_side_effects=True, vmem_limit_bytes=56 * 2**20
            ),
        )(
            perm,
            page_table,
            cache_len,
            accepted,
            parents,
            q_bias[None, :],
            norm_gain[None, :],
            norm_bias[None, :],
            fc1_bias[None, :],
            fc2_bias[None, :],
            final_gain[None, :],
            final_bias[None, :],
            tokens,
            w_query,
            w_key,
            w_value,
            w_out,
            w_fc1,
            w_fc2,
            key_pool,
            value_pool,
        )
    )


def per_device(*args):
    rows, requests = args[0].shape[0], args[1].shape[0]
    per_dev, draft = args[19].shape
    n_mdl = lax.axis_size("mdl")
    whole_positions = rows % requests == 0 and rows // requests == 8
    fits = lax.axis_size("req") == 8 and draft == 64
    if fits and whole_positions and per_dev == n_mdl == 4 and per_dev * draft == rows:
        return per_device_fused(*args)
    return per_device_general(*args)


def solution(mesh):
    in_specs = (
        P("req", "mdl"),
        P(),
        P(None, "mdl"),
        P("mdl"),
        P(None, "mdl"),
        P(None, "mdl"),
        P("mdl", None),
        P("mdl"),
        P("mdl"),
        P(None, "mdl"),
        P("mdl"),
        P("mdl", None),
        P("mdl"),
        P("mdl"),
        P("mdl"),
        P("req", None, "mdl"),
        P("req", None, "mdl"),
        P("req", None),
        P("req"),
        P("req", None),
        P("req", None),
    )
    out_specs = (P("req", "mdl"), P("req", None, "mdl"), P("req", None, "mdl"))
    return jax.shard_map(
        per_device, mesh=mesh, in_specs=in_specs, out_specs=out_specs, check_vma=False
    )
```
